256 devices in a mesh: dp: 16 (over x, y), ctx: 16 (over z, core).
Axes of the slice: x: 4, y: 4, z: 8, core: 2. Of those that a mesh axis runs over, the one named last changes fastest.
Arguments:
- hidden_in: bfloat16 [16, 2048, 1536], P('dp', 'ctx'), may hold values from -12 to 12
- cotangent: bfloat16 [16, 2048, 1536], P('dp', 'ctx'), may hold values from -0.29882812 to 0.29882812
- w_qkv: bfloat16 [3, 1536, 2048], P(None, None, 'ctx'), may hold values from -1 to 1
- w_out: bfloat16 [2048, 1536], P('ctx'), may hold values from -0.125 to 0.125
- q_gain: float32 [128], replicated, may hold values from 0.1 to 1.9
- k_gain: float32 [128], replicated, may hold values from 0.1 to 1.9
- tile_list: int32 [16, 32, 32], P('ctx'), may hold values from -1 to 31, as said below
Outputs:
- layer_out: bfloat16 [16, 2048, 1536], P('dp', 'ctx')
- grad_qkv: float32 [3, 1536, 2048], P(None, None, 'ctx')
- grad_out: float32 [2048, 1536], P('ctx')
The draws below stay inside these ranges and needn't reach their ends.
Inputs may be any that keep to these rules, and one draw needn't show every extreme that they name: tile_list[h, t] lists in increasing order the key tiles that query tile t attends to in head h, then -1 up to 32 entries. Tiles are numbered row-major over a grid of 2 x 4 x 4, tile t holding tokens t * 64 to (t + 1) * 64 - 1. Each head has a window of fixed extents in tiles along the three grid dimensions, centred on the query tile and shifted inward at the grid's edges, so that all query tiles of one head list the same number of tiles, the query tile among them. Some head's window is the whole grid.
All inputs are finite; a program needn't handle non-finite values.
Results may differ from the reference program's by a relative error of at most 0.014.
Values may be sent and summed in bfloat16 or wider, within the bound.
A program may use at most 128 MiB of HBM per device.

```python
import math
import jax
import jax.numpy as jnp
from jax import lax

D = 1536
HEADS = 16
HD = 128
GRID_T = 2
GRID_H = 4
GRID_W = 4
BLOCK = 512
NTILES = 32
SEQ = 2048
BATCH = 16


def draw_hidden_in(key, part):
    first, second = jax.random.split(key, 2)
    row_scales = jnp.exp(jax.random.uniform(second, (BATCH, SEQ, 1), jnp.float32, math.log(0.3), math.log(3.0)))
    base = jnp.clip(jax.random.normal(first, (BATCH, SEQ, D), jnp.float32), -5.0, 5.0)
    return jnp.clip(base * row_scales, -12.0, 12.0).astype(jnp.bfloat16)


def draw_w_qkv(key, part):
    first, second = jax.random.split(key, 2)
    col_scales = jnp.exp(jax.random.uniform(second, (3, 1, HEADS * HD), jnp.float32, math.log(0.3), math.log(3.0)))
    base = jnp.clip(jax.random.normal(first, (3, D, HEADS * HD), jnp.float32), -5.0, 5.0)
    return jnp.clip(base * col_scales * D ** (-0.5), -1.0, 1.0).astype(jnp.bfloat16)


def window_inside(coord, extent, length):
    lowest = jnp.clip(coord[None, :] - (extent[:, None] - 1) // 2, 0, length - extent[:, None])
    target = coord[None, None, :]
    lowest = lowest[:, :, None]
    return (target >= lowest) & (target < lowest + extent[:, None, None])


def draw_tile_list(key, part):
    first, second, third, fourth = jax.random.split(key, 4)
    heads = jnp.arange(HEADS, dtype=jnp.int32)
    widest = jax.random.randint(fourth, (), 0, HEADS)
    extent_t = jnp.where(heads == widest, GRID_T, jax.random.randint(first, (HEADS,), 1, GRID_T + 1))
    extent_h = jnp.where(heads == widest, GRID_H, jax.random.randint(second, (HEADS,), 1, GRID_H + 1))
    extent_w = jnp.where(heads == widest, GRID_W, jax.random.randint(third, (HEADS,), 1, GRID_W + 1))
    tiles = jnp.arange(NTILES, dtype=jnp.int32)
    along_t = tiles // (GRID_H * GRID_W)
    along_h = tiles // GRID_W % GRID_H
    along_w = tiles % GRID_W
    member = window_inside(along_t, extent_t, GRID_T) & window_inside(along_h, extent_h, GRID_H)
    member = member & window_inside(along_w, extent_w, GRID_W)
    ranking = jnp.where(member, tiles[None, None, :], NTILES + tiles[None, None, :])
    ordered = jnp.sort(ranking, axis=-1)
    return jnp.where(ordered < NTILES, ordered, -1).astype(jnp.int32)


def steps_of(rng, dims, pieces, smallest, largest):
    level, own = 1.0, jax.random.fold_in(rng, 6)
    for dim, shards_of in pieces:
        steps = jnp.exp(jax.random.uniform(jax.random.fold_in(own, dim), (shards_of,), jnp.float32, smallest / len(pieces), largest / len(pieces)))
        level = level * jnp.repeat(steps, dims[dim] // shards_of).reshape([-1 if axis == dim else 1 for axis in range(len(dims))])
    return level


def centred(rng, shape, width, most, shards=(), kind=jnp.bfloat16):
    factor_of = steps_of(rng, shape, shards, -0.22, 0.18) if shards else 1.0
    drawn = jax.random.normal(rng, shape, jnp.float32) * width * factor_of
    return jnp.minimum(jnp.maximum(drawn, -most), most).astype(kind)


def setup_inputs(seed: int = 0) -> dict:
    keys = jax.random.split(jax.random.key(seed), 8)
    hidden_in = draw_hidden_in(jax.random.fold_in(keys[7], 71), 0)
    cotangent = centred(keys[1], (BATCH, SEQ, D), 0.05, 0.29882812, ((0, 16), (1, 16)))
    w_qkv = draw_w_qkv(jax.random.fold_in(keys[7], 71), 0)
    w_out = centred(keys[3], (HEADS * HD, D), (HEADS * HD) ** -0.5, 0.125, ((0, 16),))
    q_gain = jnp.clip(1.0 + 0.18 * jax.random.normal(keys[4], (HD,), jnp.float32), 0.1, 1.9)
    k_gain = jnp.clip(1.0 + 0.18 * jax.random.normal(keys[5], (HD,), jnp.float32), 0.1, 1.9)
    tile_list = draw_tile_list(jax.random.fold_in(keys[7], 71), 0)
    return dict(hidden_in=hidden_in, cotangent=cotangent, w_qkv=w_qkv, w_out=w_out, q_gain=q_gain, k_gain=k_gain, tile_list=tile_list)


EPS = 1e-06

def tile_allowed(lists, tile_count):
    match = lists[:, :, None] == jnp.arange(tile_count, dtype=jnp.int32)[None, None, :]
    return jnp.any(match, axis=1).astype(jnp.float32)

def expand_rows(allowed_rows, tile_rows):
    return jnp.repeat(jnp.repeat(allowed_rows, tile_rows, axis=0), tile_rows, axis=1)

def rms_forward(raw, gain):
    inverse = lax.rsqrt(lax.optimization_barrier(jnp.mean(raw * raw, axis=-1, keepdims=True)) + EPS)
    return ((raw * inverse * gain).astype(jnp.bfloat16), inverse)

def rms_backward(raw, inverse, gain, upstream):
    normed = raw * inverse
    scaled = gain * upstream
    return (inverse * (scaled - normed * lax.optimization_barrier(jnp.mean(normed * scaled, axis=-1, keepdims=True)))).astype(jnp.bfloat16)

def contract(left, right, left_dim, right_dim):
    return lax.dot_general(left, right, (((left_dim,), (right_dim,)), ((), ())), preferred_element_type=jnp.float32)

def head_reference(tokens, upstream, w_query, w_key, w_value, w_proj, q_gain, k_gain, allowed):
    seq_len = tokens.shape[0]
    head_size = w_query.shape[1]
    tile_rows = seq_len // allowed.shape[0]
    block_tiles = BLOCK // tile_rows
    score_scale = head_size ** (-0.5)
    query_raw = jnp.dot(tokens, w_query, preferred_element_type=jnp.float32)
    key_raw = jnp.dot(tokens, w_key, preferred_element_type=jnp.float32)
    value_raw = jnp.dot(tokens, w_value, preferred_element_type=jnp.float32)
    query_normed, query_inverse = rms_forward(query_raw, q_gain)
    key_normed, key_inverse = rms_forward(key_raw, k_gain)
    values = value_raw.astype(jnp.bfloat16)
    d_attention = contract(upstream, w_proj, 1, 1).astype(jnp.bfloat16)

    def step(running, index):
        key_grad, value_grad = running
        offset = index * BLOCK
        query_block = lax.dynamic_slice_in_dim(query_normed, offset, BLOCK, 0)
        allowed_block = expand_rows(lax.dynamic_slice_in_dim(allowed, index * block_tiles, block_tiles, 0), tile_rows)
        scores = contract(query_block, key_normed, 1, 1) * score_scale
        weighted = jnp.exp(scores) * allowed_block
        probabilities = weighted / lax.optimization_barrier(jnp.sum(weighted, axis=-1, keepdims=True))
        weights_bf = probabilities.astype(jnp.bfloat16)
        attn_block = jnp.dot(weights_bf, values, preferred_element_type=jnp.float32).astype(jnp.bfloat16)
        upstream_block = lax.dynamic_slice_in_dim(d_attention, offset, BLOCK, 0)
        weight_grad = contract(upstream_block, values, 1, 1)
        value_grad = value_grad + contract(weights_bf, upstream_block, 0, 0)
        row_delta = lax.optimization_barrier(jnp.sum(probabilities * weight_grad, axis=-1, keepdims=True))
        score_grad = (probabilities * (weight_grad - row_delta) * score_scale).astype(jnp.bfloat16)
        query_grad = jnp.dot(score_grad, key_normed, preferred_element_type=jnp.float32)
        key_grad = key_grad + contract(score_grad, query_block, 0, 0)
        return ((key_grad, value_grad), (attn_block, query_grad))
    zeros = jnp.zeros((seq_len, head_size), jnp.float32)
    (key_grad, value_grad), (attn_blocks, query_grads) = lax.scan(step, (zeros, zeros), jnp.arange(seq_len // BLOCK, dtype=jnp.int32))
    attention = attn_blocks.reshape(seq_len, head_size)
    query_grad = query_grads.reshape(seq_len, head_size)
    query_back = rms_backward(query_raw, query_inverse, q_gain, query_grad)
    key_back = rms_backward(key_raw, key_inverse, k_gain, key_grad)
    value_back = value_grad.astype(jnp.bfloat16)
    grads = jnp.stack([contract(tokens, query_back, 0, 0), contract(tokens, key_back, 0, 0), contract(tokens, value_back, 0, 0)])
    proj_grad = contract(attention, upstream, 0, 0)
    partial_out = jnp.dot(attention, w_proj, preferred_element_type=jnp.float32)
    return (partial_out, grads, proj_grad)

def reference(hidden_in, cotangent, w_qkv, w_out, q_gain, k_gain, tile_list):

    def clip_pass(running, sample):
        tokens, upstream = sample

        def head_pass(out_sum, head):
            low_col = head * HD
            w_query = lax.dynamic_slice_in_dim(w_qkv[0], low_col, HD, 1)
            w_key = lax.dynamic_slice_in_dim(w_qkv[1], low_col, HD, 1)
            w_value = lax.dynamic_slice_in_dim(w_qkv[2], low_col, HD, 1)
            w_proj = lax.dynamic_slice_in_dim(w_out, low_col, HD, 0)
            allowed = tile_allowed(tile_list[head], NTILES)
            partial_out, grads, proj_grad = head_reference(tokens, upstream, w_query, w_key, w_value, w_proj, q_gain, k_gain, allowed)
            return (out_sum + partial_out, (grads, proj_grad))
        out_sum, (grads, proj_grads) = lax.scan(head_pass, jnp.zeros((SEQ, D), jnp.float32), jnp.arange(HEADS, dtype=jnp.int32))
        qkv_sum, proj_sum = running
        return ((qkv_sum + grads, proj_sum + proj_grads), out_sum.astype(jnp.bfloat16))
    initial = (jnp.zeros((HEADS, 3, D, HD), jnp.float32), jnp.zeros((HEADS, HD, D), jnp.float32))
    (qkv_sum, proj_sum), outputs = lax.scan(clip_pass, initial, (hidden_in, cotangent))
    grad_qkv = jnp.transpose(qkv_sum, (1, 2, 0, 3)).reshape(3, D, HEADS * HD)
    grad_out = proj_sum.reshape(HEADS * HD, D)
    return (outputs, grad_qkv, grad_out)
```

```python
import functools
import jax
import jax.numpy as jnp
from jax.sharding import PartitionSpec as P
from jax import lax
from jax.experimental import pallas as pl
from jax.experimental.pallas import tpu as pltpu
EPS=1e-6
F32=jnp.float32; BF=jnp.bfloat16
def mm(a,b,ca=1,cb=0):
    return lax.dot_general(a,b,(((ca,),(cb,)),((),())),preferred_element_type=F32)

def qkv_block(row, rows, tok, w, gq, gk, qraw, kraw, qn, kn, va, tile_rows):
    x=tok[pl.ds(row,rows),:]
    r=mm(x,w[...])
    hd=gq.shape[1]
    q=r[:,:hd]; k=r[:,hd:2*hd]; v=r[:,2*hd:]
    qraw[pl.ds(row,rows),:]=q
    kraw[pl.ds(row,rows),:]=k
    rq=lax.rsqrt(jnp.mean(q*q,axis=-1,keepdims=True)+EPS)
    rk=lax.rsqrt(jnp.mean(k*k,axis=-1,keepdims=True)+EPS)
    qn[pl.ds(row,rows),:hd]=(q*rq*gq[...]).astype(BF)
    kn[pl.ds(row,rows),:hd]=(k*rk*gk[...]).astype(BF)
    va[pl.ds(row,rows),:hd]=v.astype(BF)
    va[pl.ds(row,rows),hd:]=jnp.ones((rows,hd),BF)
    t=(row+lax.broadcasted_iota(jnp.int32,(rows,hd),0))//tile_rows
    lane=lax.broadcasted_iota(jnp.int32,(rows,hd),1)
    qn[pl.ds(row,rows),hd:]=jnp.where(t==lane,1.0,0.0).astype(BF)

def rms_back(raw,gain,up,axis):
    inv=lax.rsqrt(jnp.mean(raw*raw,axis=axis,keepdims=True)+EPS)
    n=raw*inv
    s=gain*up
    return inv*(s-n*jnp.mean(n*s,axis=axis,keepdims=True))

def attn_block(row, rows, first, scale, qn, kn, va, dA, qraw, gq, att, gl, dkt, dvt):
    hd=gq.shape[1]
    L2E=1.4426950408889634
    qb=qn[pl.ds(row,rows),:]
    s=mm(qb,kn[...],1,1)
    e=jnp.exp2(s*(scale*L2E))
    eb=e.astype(BF)
    av=mm(eb,va[...])
    inv=1.0/av[:,hd:]
    a=av[:,:hd]*inv
    att[pl.ds(row,rows),:]=a.astype(BF)
    da=dA[pl.ds(row,rows),:].astype(F32)
    delta=-jnp.sum(da*a,axis=-1,keepdims=True)*inv
    hi=delta.astype(BF).astype(F32)
    lane=lax.broadcasted_iota(jnp.int32,(rows,hd),1)
    tail=jnp.where(lane==0,hi,jnp.where(lane==1,delta-hi,0.0)).astype(BF)
    das=(da*inv).astype(BF)
    dw=mm(jnp.concatenate([das,tail],axis=1),va[...],1,1)
    ds=(e*dw).astype(BF)
    dq=mm(ds,kn[:,:hd])*scale
    dk=mm(qb[:,:hd],ds,0,0)
    dv=mm(das,eb,0,0)
    dkt[...]+=dk
    dvt[...]+=dv
    dqr=rms_back(qraw[pl.ds(row,rows),:],gq[...],dq,-1)
    gl[0:hd,pl.ds(row,rows)]=jnp.transpose(dqr).astype(BF)

def finish(scale, kraw, gkc, dkt, dvt, gl):
    hd=dkt.shape[0]
    seq=dkt.shape[1]
    step=512
    @pl.loop(0,seq//step)
    def _(i):
        c=pl.multiple_of(i*step,step)
        kt=jnp.transpose(kraw[pl.ds(c,step),:])
        r=rms_back(kt,gkc[...],dkt[:,pl.ds(c,step)]*scale,0)
        gl[hd:2*hd,pl.ds(c,step)]=r.astype(BF)
        gl[2*hd:,pl.ds(c,step)]=dvt[:,pl.ds(c,step)].astype(BF)

def local_kernel(scale, tile_rows, tok_h, cot_h, w, wo, gq, gk, gkc, kb,
                 att_o, g_o, tok, cot, qraw, kraw, qn, kn, va, dA, gl, dkt, dvt, sem):
    seq=tok.shape[0]; hd=gq.shape[1]; R=256; nb=seq//R
    cps=[]
    for j,(h,v) in enumerate(((tok_h,tok),(cot_h,cot))):
        for i in range(nb):
            c=pltpu.make_async_copy(h.at[pl.ds(i*R,R)],v.at[pl.ds(i*R,R)],sem.at[j,i]); c.start(); cps.append(c)
    kn[:,hd:]=kb[...]
    dkt[...]=jnp.zeros_like(dkt); dvt[...]=jnp.zeros_like(dvt)
    for c in cps: c.wait()
    @pl.loop(0,nb)
    def _(i):
        row=pl.multiple_of(i*R,R)
        qkv_block(row,R,tok,w,gq,gk,qraw,kraw,qn,kn,va,tile_rows)
        dA[pl.ds(row,R),:]=mm(cot[pl.ds(row,R),:],wo[...],1,1).astype(BF)
    @pl.loop(0,nb)
    def _(i):
        row=pl.multiple_of(i*R,R)
        attn_block(row,R,None,scale,qn,kn,va,dA,qraw,gq,att_o,gl,dkt,dvt)
    finish(scale,kraw,gkc,dkt,dvt,gl)
    N=256
    @pl.loop(0,tok.shape[1]//N)
    def _(i):
        c=pl.multiple_of(i*N,N)
        g_o[:3*hd,pl.ds(c,N)]=mm(gl[...],tok[:,pl.ds(c,N)]).astype(BF)
        g_o[3*hd:,pl.ds(c,N)]=mm(att_o[...],cot[:,pl.ds(c,N)],0,0).astype(BF)

def local_call(tokens,cot,w,wo,q_gain,k_gain,allowed):
    seq,D=tokens.shape; hd=q_gain.shape[0]
    tile_rows=seq//allowed.shape[0]
    bias=jnp.where(allowed>0.5,0.0,-30000.0).astype(BF)
    kb=jnp.pad(jnp.repeat(bias.T,tile_rows,axis=0),((0,0),(0,hd-allowed.shape[0])))
    V=pl.BlockSpec(memory_space=pltpu.VMEM); A=pl.BlockSpec(memory_space=pl.ANY)
    nb=seq//256
    return pl.pallas_call(functools.partial(local_kernel,hd**-0.5,tile_rows),
      out_shape=(jax.ShapeDtypeStruct((seq,hd),BF),jax.ShapeDtypeStruct((4*hd,D),BF)),
      in_specs=[A,A]+[V]*6, out_specs=(V,V),
      scratch_shapes=[pltpu.VMEM((seq,D),BF)]*2+[pltpu.VMEM((seq,hd),F32)]*2+[pltpu.VMEM((seq,2*hd),BF)]*3
       +[pltpu.VMEM((seq,hd),BF),pltpu.VMEM((3*hd,seq),BF),pltpu.VMEM((hd,seq),F32),pltpu.VMEM((hd,seq),F32),pltpu.SemaphoreType.DMA((2,nb))],
      compiler_params=pltpu.CompilerParams(vmem_limit_bytes=60*1024*1024),
    )(tokens,cot,w,wo,q_gain[None],k_gain[None],k_gain[:,None],kb)


def exchange_kernel(n, att, w, out, rows, send, recv, own):
    me = lax.axis_index("ctx"); dp = lax.axis_index("dp")
    T = rows.shape[0]; hd = att.shape[1]
    bar = pltpu.get_barrier_semaphore()
    def peer(k):
        return lax.rem(me + k, n)
    for k in range(1, n):
        pl.semaphore_signal(bar, inc=1, device_id=(dp, peer(k)), device_id_type=pl.DeviceIdType.MESH)
    pl.semaphore_wait(bar, n - 1)
    def copy(k):
        p = peer(k)
        return pltpu.make_async_remote_copy(
            src_ref=att.at[pl.ds(pl.multiple_of(p * T, T), T)],
            dst_ref=rows.at[:, pl.ds(pl.multiple_of(me * hd, hd), hd)],
            send_sem=send.at[k], recv_sem=recv.at[k],
            device_id=(dp, p), device_id_type=pl.DeviceIdType.MESH)
    for k in range(1, n):
        copy(k).start()
    mine = pltpu.make_async_copy(att.at[pl.ds(pl.multiple_of(me * T, T), T)],
                                 rows.at[:, pl.ds(pl.multiple_of(me * hd, hd), hd)], own)
    mine.start()
    mine.wait()
    for k in range(1, n):
        copy(k).wait()
    out[...] = mm(rows[...], w[...]).astype(BF)


def exchange_call(att, w_full, n):
    seq, hd = att.shape
    V = pl.BlockSpec(memory_space=pltpu.VMEM)
    return pl.pallas_call(functools.partial(exchange_kernel, n),
        out_shape=jax.ShapeDtypeStruct((seq // n, w_full.shape[1]), BF),
        in_specs=[pl.BlockSpec(memory_space=pl.ANY), V], out_specs=V,
        scratch_shapes=[pltpu.VMEM((seq // n, n * hd), BF), pltpu.SemaphoreType.DMA((n,)),
                        pltpu.SemaphoreType.DMA((n,)), pltpu.SemaphoreType.DMA],
        compiler_params=pltpu.CompilerParams(collective_id=1, has_side_effects=True, vmem_limit_bytes=40 * 1024 * 1024),
    )(att, w_full)


def tile_allowed(lists, tile_count):
    match = lists[:, :, None] == jnp.arange(tile_count, dtype=jnp.int32)[None, None, :]
    return jnp.any(match, axis=1).astype(jnp.float32)


def per_device(n, hidden_in, cotangent, w_qkv, w_out, q_gain, k_gain, tile_list):
    tokens = lax.all_gather(hidden_in[0], "ctx", axis=0, tiled=True)
    upstream = lax.all_gather(cotangent[0], "ctx", axis=0, tiled=True)
    w_full = lax.all_gather(w_out, "ctx", axis=0, tiled=True)
    allowed = tile_allowed(tile_list[0], tile_list.shape[1])
    w = jnp.concatenate([w_qkv[0], w_qkv[1], w_qkv[2]], axis=1)
    att, g = local_call(tokens, upstream, w, w_out, q_gain, k_gain, allowed)
    g = lax.psum(g, "dp")
    layer = exchange_call(att, w_full, n)
    hd = q_gain.shape[0]
    gq = g[:3 * hd].reshape(3, hd, -1).transpose(0, 2, 1).astype(F32)
    return layer[None], gq, g[3 * hd:].astype(F32)


def solution(mesh):
    in_specs = (
        P("dp", "ctx", None),
        P("dp", "ctx", None),
        P(None, None, "ctx"),
        P("ctx", None),
        P(),
        P(),
        P("ctx", None, None),
    )
    out_specs = (P("dp", "ctx", None), P(None, None, "ctx"), P("ctx", None))
    return jax.shard_map(
        functools.partial(per_device, mesh.shape["ctx"]), mesh=mesh, in_specs=in_specs, out_specs=out_specs, check_vma=False
    )
```

```python
import functools
import jax
import jax.numpy as jnp
from jax.sharding import PartitionSpec as P
from jax import lax
from jax.experimental import pallas as pl
from jax.experimental.pallas import tpu as pltpu
EPS=1e-6
F32=jnp.float32; BF=jnp.bfloat16
def mm(a,b,ca=1,cb=0):
    return lax.dot_general(a,b,(((ca,),(cb,)),((),())),preferred_element_type=F32)

def qkv_block(row, rows, tok, w, gq, gk, qraw, kraw, qn, kn, va, tile_rows):
    x=tok[pl.ds(row,rows),:]
    r=mm(x,w[...])
    hd=gq.shape[1]
    q=r[:,:hd]; k=r[:,hd:2*hd]; v=r[:,2*hd:]
    qraw[pl.ds(row,rows),:]=q
    kraw[pl.ds(row,rows),:]=k
    rq=lax.rsqrt(jnp.mean(q*q,axis=-1,keepdims=True)+EPS)
    rk=lax.rsqrt(jnp.mean(k*k,axis=-1,keepdims=True)+EPS)
    qn[pl.ds(row,rows),:hd]=(q*rq*gq[...]).astype(BF)
    kn[pl.ds(row,rows),:hd]=(k*rk*gk[...]).astype(BF)
    va[pl.ds(row,rows),:hd]=v.astype(BF)
    va[pl.ds(row,rows),hd:]=jnp.ones((rows,hd),BF)
    t=(row+lax.broadcasted_iota(jnp.int32,(rows,hd),0))//tile_rows
    lane=lax.broadcasted_iota(jnp.int32,(rows,hd),1)
    qn[pl.ds(row,rows),hd:]=jnp.where(t==lane,1.0,0.0).astype(BF)

def rms_back(raw,gain,up,axis):
    inv=lax.rsqrt(jnp.mean(raw*raw,axis=axis,keepdims=True)+EPS)
    n=raw*inv
    s=gain*up
    return inv*(s-n*jnp.mean(n*s,axis=axis,keepdims=True))

def attn_block(row, rows, first, scale, qn, kn, va, dA, qraw, gq, att, gl, dkt, dvt):
    hd=gq.shape[1]
    L2E=1.4426950408889634
    qb=qn[pl.ds(row,rows),:]
    s=mm(qb,kn[...],1,1)
    e=jnp.exp2(s*(scale*L2E))
    eb=e.astype(BF)
    av=mm(eb,va[...])
    inv=1.0/av[:,hd:]
    a=av[:,:hd]*inv
    att[pl.ds(row,rows),:]=a.astype(BF)
    da=dA[pl.ds(row,rows),:].astype(F32)
    delta=-jnp.sum(da*a,axis=-1,keepdims=True)*inv
    hi=delta.astype(BF).astype(F32)
    lane=lax.broadcasted_iota(jnp.int32,(rows,hd),1)
    tail=jnp.where(lane==0,hi,jnp.where(lane==1,delta-hi,0.0)).astype(BF)
    das=(da*inv).astype(BF)
    dw=mm(jnp.concatenate([das,tail],axis=1),va[...],1,1)
    ds=(e*dw).astype(BF)
    dq=mm(ds,kn[:,:hd])*scale
    dk=mm(qb[:,:hd],ds,0,0)
    dv=mm(das,eb,0,0)
    dkt[...]+=dk
    dvt[...]+=dv
    dqr=rms_back(qraw[pl.ds(row,rows),:],gq[...],dq,-1)
    gl[0:hd,pl.ds(row,rows)]=jnp.transpose(dqr).astype(BF)

def finish(scale, kraw, gkc, dkt, dvt, gl):
    hd=dkt.shape[0]
    seq=dkt.shape[1]
    step=512
    @pl.loop(0,seq//step)
    def _(i):
        c=pl.multiple_of(i*step,step)
        kt=jnp.transpose(kraw[pl.ds(c,step),:])
        r=rms_back(kt,gkc[...],dkt[:,pl.ds(c,step)]*scale,0)
        gl[hd:2*hd,pl.ds(c,step)]=r.astype(BF)
        gl[2*hd:,pl.ds(c,step)]=dvt[:,pl.ds(c,step)].astype(BF)

def mesh_copy(src, dst, send, recv, target):
    return pltpu.make_async_remote_copy(
        src_ref=src, dst_ref=dst, send_sem=send, recv_sem=recv,
        device_id=target, device_id_type=pl.DeviceIdType.MESH)


def layer_kernel(scale, n, tok_h, cot_h, w3, wo, gq, gk, tiles, att_o, g_o,
                 tok, cot, w, qraw, kraw, qn, kn, va, dA, gl, dkt, dvt,
                 ring_send, ring_recv, sib_send, sib_recv, own_send, own_recv, local):
    chips = n // 2
    own = tok_h.shape[0]
    chip = 2 * own
    half = own // 2
    events = chips - 1
    hd = gq.shape[1]
    tile_rows = tok.shape[0] // tiles.shape[0]
    me = lax.axis_index("ctx")
    dp = lax.axis_index("dp")
    z = me // 2
    c = me % 2
    sib = (dp, me + 1 - 2 * c)
    side = ((dp, lax.rem(me + 2, n)), (dp, lax.rem(me + n - 2, n)))
    bar = pltpu.get_barrier_semaphore()
    for t in (sib,) + side:
        pl.semaphore_signal(bar, inc=1, device_id=t, device_id_type=pl.DeviceIdType.MESH)
    pl.semaphore_wait(bar, 3)

    def chunk(way, e, core):
        far = e // 2 + 1
        part = e % 2
        origin = lax.rem(z + (chips - far if way == 0 else far), chips)
        return pl.ds(pl.multiple_of(origin * chip + core * own + (part if way == 0 else 1 - part) * half, half), half)

    heads = (tok_h, cot_h)
    bufs = (tok, cot)

    def sent(s, way, e):
        return mesh_copy(bufs[s].at[chunk(way, e - 2, c)], bufs[s].at[chunk(way, e - 2, c)],
                         ring_send.at[s, way, e], ring_recv.at[s, way, e], side[way])

    def first(s, way, e):
        h = e if way == 0 else 1 - e
        return mesh_copy(heads[s].at[pl.ds(h * half, half)],
                         bufs[s].at[pl.ds(pl.multiple_of(me * own + h * half, half), half)],
                         ring_send.at[s, way, e], ring_recv.at[s, way, e], side[way])

    def shared(s, way, e):
        return mesh_copy(bufs[s].at[chunk(way, e, c)], bufs[s].at[chunk(way, e, c)],
                         sib_send.at[s, way, e], sib_recv.at[s, way, e], sib)

    place = pl.ds(pl.multiple_of(me * own, own), own)

    def lodged(s):
        return mesh_copy(heads[s], bufs[s].at[place], own_send.at[s], own_recv.at[s], sib)

    def kept(s):
        return pltpu.make_async_copy(heads[s], bufs[s].at[place], local.at[s])

    def begin(s):
        for e in (0, 1):
            for way in (0, 1):
                first(s, way, e).start()
        lodged(s).start()
        kept(s).start()

    def event(s, i):
        @pl.when(i < events)
        def _():
            for way in (0, 1):
                mesh_copy(bufs[s].at[chunk(way, i, c)], bufs[s].at[chunk(way, i, c)],
                          ring_send.at[s, way, i], ring_recv.at[s, way, i], side[way]).wait_recv()

                @pl.when(i < events - 2)
                def _():
                    sent(s, way, i + 2).start()
                shared(s, way, i).start()

    def block_row(s, i):
        far = (i + 1) // 2

        @pl.when(i == 0)
        def _():
            lodged(s).wait_recv()
            kept(s).wait()

        for way in (0, 1):
            @pl.when(jnp.logical_and(i % 2 == 1 - way, jnp.logical_and(i > 0, i < chips - 1)))
            def _():
                shared(s, way, 2 * far - 2).wait_recv()
                shared(s, way, 2 * far - 1).wait_recv()

            @pl.when(i == chips - 1)
            def _():
                shared(s, way, events - 1).wait_recv()
        zc = lax.rem(z + jnp.where(i % 2 == 1, chips - far, far), chips)
        return pl.multiple_of(zc * chip, chip)

    begin(0)
    for j in range(3):
        w[:, j * hd:(j + 1) * hd] = w3[j]
    lists = tiles[...]
    lane = lax.broadcasted_iota(jnp.int32, (hd, hd), 1)
    count = lists.shape[0]
    hit = jnp.zeros((count, hd), jnp.bool_)
    for j in range(lists.shape[1]):
        hit = jnp.logical_or(hit, lists[:, j:j + 1] == lane[:count])
    bias = jnp.where(hit, 0.0, -30000.0)
    bias = jnp.transpose(jnp.concatenate([bias, jnp.zeros((hd - count, hd), F32)], axis=0))
    for j in range(count):
        kn[j * tile_rows:(j + 1) * tile_rows, hd:] = jnp.broadcast_to(bias[j:j + 1, :], (tile_rows, hd)).astype(BF)
    dkt[...] = jnp.zeros_like(dkt)
    dvt[...] = jnp.zeros_like(dvt)

    @pl.loop(0, chips)
    def _(i):
        event(0, i)

        @pl.when(i == events - 3)
        def _():
            begin(1)
        row = block_row(0, i)
        qkv_block(row, chip, tok, w, gq, gk, qraw, kraw, qn, kn, va, tile_rows)

    @pl.loop(0, chips)
    def _(i):
        event(1, i)
        row = block_row(1, i)
        dA[pl.ds(row, chip), :] = mm(cot[pl.ds(row, chip), :], wo[...], 1, 1).astype(BF)
        attn_block(row, chip, None, scale, qn, kn, va, dA, qraw, gq, att_o, gl, dkt, dvt)

    gkc = jnp.transpose(jnp.broadcast_to(gk[...], (hd, hd)))[:, :1]
    finish(scale, kraw, gkc, dkt, dvt, gl)
    N = 256

    @pl.loop(0, tok.shape[1] // N)
    def _(i):
        col = pl.multiple_of(i * N, N)
        g_o[:3 * hd, pl.ds(col, N)] = mm(gl[...], tok[:, pl.ds(col, N)]).astype(BF)
        g_o[3 * hd:, pl.ds(col, N)] = mm(att_o[...], cot[:, pl.ds(col, N)], 0, 0).astype(BF)

    for s in (0, 1):
        lodged(s).wait_send()
        for way in (0, 1):
            for e in range(events):
                (first if e < 2 else sent)(s, way, e).wait_send()
                shared(s, way, e).wait_send()


def layer_call(n, hidden, cot, w3, wo, q_gain, k_gain, tiles):
    own, D = hidden.shape
    seq = own * n
    hd = q_gain.shape[0]
    V = pl.BlockSpec(memory_space=pltpu.VMEM)
    A = pl.BlockSpec(memory_space=pl.ANY)
    dma = pltpu.SemaphoreType.DMA
    e = n // 2 - 1
    return pl.pallas_call(
        functools.partial(layer_kernel, hd ** -0.5, n),
        out_shape=(jax.ShapeDtypeStruct((seq, hd), BF), jax.ShapeDtypeStruct((4 * hd, D), BF)),
        in_specs=[A, A] + [V] * 5, out_specs=(V, V),
        scratch_shapes=[pltpu.VMEM((seq, D), BF)] * 2 + [pltpu.VMEM((D, 3 * hd), BF)]
        + [pltpu.VMEM((seq, hd), F32)] * 2 + [pltpu.VMEM((seq, 2 * hd), BF)] * 3
        + [pltpu.VMEM((seq, hd), BF), pltpu.VMEM((3 * hd, seq), BF)] + [pltpu.VMEM((hd, seq), F32)] * 2
        + [dma((2, 2, e))] * 4 + [dma((2,))] * 3,
        compiler_params=pltpu.CompilerParams(collective_id=2, has_side_effects=True, vmem_limit_bytes=60 * 1024 * 1024),
    )(hidden, cot, w3, wo, q_gain[None], k_gain[None], tiles)


def exchange_kernel(n, att, w, out, rows, send, recv, own):
    me = lax.axis_index("ctx"); dp = lax.axis_index("dp")
    T = rows.shape[0]; hd = att.shape[1]
    bar = pltpu.get_barrier_semaphore()
    def peer(k):
        return lax.rem(me + k, n)
    for k in range(1, n):
        pl.semaphore_signal(bar, inc=1, device_id=(dp, peer(k)), device_id_type=pl.DeviceIdType.MESH)
    pl.semaphore_wait(bar, n - 1)
    def copy(k):
        p = peer(k)
        return pltpu.make_async_remote_copy(
            src_ref=att.at[pl.ds(pl.multiple_of(p * T, T), T)],
            dst_ref=rows.at[:, pl.ds(pl.multiple_of(me * hd, hd), hd)],
            send_sem=send.at[k], recv_sem=recv.at[k],
            device_id=(dp, p), device_id_type=pl.DeviceIdType.MESH)
    for k in range(1, n):
        copy(k).start()
    mine = pltpu.make_async_copy(att.at[pl.ds(pl.multiple_of(me * T, T), T)],
                                 rows.at[:, pl.ds(pl.multiple_of(me * hd, hd), hd)], own)
    mine.start()
    mine.wait()
    for k in range(1, n):
        copy(k).wait()
    out[...] = mm(rows[...], w[...]).astype(BF)


def exchange_call(att, w_full, n):
    seq, hd = att.shape
    V = pl.BlockSpec(memory_space=pltpu.VMEM)
    return pl.pallas_call(functools.partial(exchange_kernel, n),
        out_shape=jax.ShapeDtypeStruct((seq // n, w_full.shape[1]), BF),
        in_specs=[pl.BlockSpec(memory_space=pl.ANY), V], out_specs=V,
        scratch_shapes=[pltpu.VMEM((seq // n, n * hd), BF), pltpu.SemaphoreType.DMA((n,)),
                        pltpu.SemaphoreType.DMA((n,)), pltpu.SemaphoreType.DMA],
        compiler_params=pltpu.CompilerParams(collective_id=1, has_side_effects=True, vmem_limit_bytes=40 * 1024 * 1024),
    )(att, w_full)


def per_device(n, hidden_in, cotangent, w_qkv, w_out, q_gain, k_gain, tile_list):
    w_full = lax.all_gather(w_out, "ctx", axis=0, tiled=True)
    att, g = layer_call(n, hidden_in[0], cotangent[0], w_qkv, w_out, q_gain, k_gain, tile_list[0])
    g = lax.psum(g, "dp")
    layer = exchange_call(att, w_full, n)
    hd = q_gain.shape[0]
    gq = g[:3 * hd].reshape(3, hd, -1).transpose(0, 2, 1).astype(F32)
    return layer[None], gq, g[3 * hd:].astype(F32)


def solution(mesh):
    in_specs = (
        P("dp", "ctx", None),
        P("dp", "ctx", None),
        P(None, None, "ctx"),
        P("ctx", None),
        P(),
        P(),
        P("ctx", None, None),
    )
    out_specs = (P("dp", "ctx", None), P(None, None, "ctx"), P("ctx", None))
    return jax.shard_map(
        functools.partial(per_device, mesh.shape["ctx"]), mesh=mesh, in_specs=in_specs, out_specs=out_specs, check_vma=False
    )
```

```python
import functools
import jax
import jax.numpy as jnp
from jax.sharding import PartitionSpec as P
from jax import lax
from jax.experimental import pallas as pl
from jax.experimental.pallas import tpu as pltpu
EPS=1e-6
F32=jnp.float32; BF=jnp.bfloat16
def mm(a,b,ca=1,cb=0):
    return lax.dot_general(a,b,(((ca,),(cb,)),((),())),preferred_element_type=F32)

def qkv_block(row, rows, tok, w, gq, gk, qraw, kraw, qn, kn, va, tile_rows):
    x=tok[pl.ds(row,rows),:]
    r=mm(x,w[...])
    hd=gq.shape[1]
    q=r[:,:hd]; k=r[:,hd:2*hd]; v=r[:,2*hd:]
    qraw[pl.ds(row,rows),:]=q
    kraw[pl.ds(row,rows),:]=k
    rq=lax.rsqrt(jnp.mean(q*q,axis=-1,keepdims=True)+EPS)
    rk=lax.rsqrt(jnp.mean(k*k,axis=-1,keepdims=True)+EPS)
    qn[pl.ds(row,rows),:hd]=(q*rq*gq[...]).astype(BF)
    kn[pl.ds(row,rows),:hd]=(k*rk*gk[...]).astype(BF)
    va[pl.ds(row,rows),:hd]=v.astype(BF)
    va[pl.ds(row,rows),hd:]=jnp.ones((rows,hd),BF)
    t=(row+lax.broadcasted_iota(jnp.int32,(rows,hd),0))//tile_rows
    lane=lax.broadcasted_iota(jnp.int32,(rows,hd),1)
    qn[pl.ds(row,rows),hd:]=jnp.where(t==lane,1.0,0.0).astype(BF)

def rms_back(raw,gain,up,axis):
    inv=lax.rsqrt(jnp.mean(raw*raw,axis=axis,keepdims=True)+EPS)
    n=raw*inv
    s=gain*up
    return inv*(s-n*jnp.mean(n*s,axis=axis,keepdims=True))

def attn_block(row, rows, first, scale, qn, kn, va, dA, qraw, gq, att, gl, dkt, dvt):
    hd=gq.shape[1]
    L2E=1.4426950408889634
    qb=qn[pl.ds(row,rows),:]
    s=mm(qb,kn[...],1,1)
    e=jnp.exp2(s*(scale*L2E))
    eb=e.astype(BF)
    av=mm(eb,va[...])
    inv=1.0/av[:,hd:]
    a=av[:,:hd]*inv
    att[pl.ds(row,rows),:]=a.astype(BF)
    da=dA[pl.ds(row,rows),:].astype(F32)
    delta=-jnp.sum(da*a,axis=-1,keepdims=True)*inv
    hi=delta.astype(BF).astype(F32)
    lane=lax.broadcasted_iota(jnp.int32,(rows,hd),1)
    tail=jnp.where(lane==0,hi,jnp.where(lane==1,delta-hi,0.0)).astype(BF)
    das=(da*inv).astype(BF)
    dw=mm(jnp.concatenate([das,tail],axis=1),va[...],1,1)
    ds=(e*dw).astype(BF)
    dq=mm(ds,kn[:,:hd])*scale
    dk=mm(qb[:,:hd],ds,0,0)
    dv=mm(das,eb,0,0)
    dkt[...]+=dk
    dvt[...]+=dv
    dqr=rms_back(qraw[pl.ds(row,rows),:],gq[...],dq,-1)
    gl[0:hd,pl.ds(row,rows)]=jnp.transpose(dqr).astype(BF)

def finish(scale, kraw, gkc, dkt, dvt, gl):
    hd=dkt.shape[0]
    seq=dkt.shape[1]
    step=512
    @pl.loop(0,seq//step)
    def _(i):
        c=pl.multiple_of(i*step,step)
        kt=jnp.transpose(kraw[pl.ds(c,step),:])
        r=rms_back(kt,gkc[...],dkt[:,pl.ds(c,step)]*scale,0)
        gl[hd:2*hd,pl.ds(c,step)]=r.astype(BF)
        gl[2*hd:,pl.ds(c,step)]=dvt[:,pl.ds(c,step)].astype(BF)

def mesh_copy(src, dst, send, recv, target):
    return pltpu.make_async_remote_copy(
        src_ref=src, dst_ref=dst, send_sem=send, recv_sem=recv,
        device_id=target, device_id_type=pl.DeviceIdType.MESH)


def layer_kernel(scale, n, tok_h, cot_h, w3, wo, gq, gk, tiles, att_o, g_o,
                 tok, cot, w, qraw, kraw, qn, kn, va, dA, gl, dkt, dvt,
                 ring_send, ring_recv, sib_send, sib_recv, own_send, own_recv, local):
    chips = n // 2
    own = tok_h.shape[0]
    chip = 2 * own
    half = own // 2
    events = chips - 1
    hd = gq.shape[1]
    tile_rows = tok.shape[0] // tiles.shape[0]
    me = lax.axis_index("ctx")
    dp = lax.axis_index("dp")
    z = me // 2
    c = me % 2
    sib = (dp, me + 1 - 2 * c)
    side = ((dp, lax.rem(me + 2, n)), (dp, lax.rem(me + n - 2, n)))
    bar = pltpu.get_barrier_semaphore()
    for t in (sib,) + side:
        pl.semaphore_signal(bar, inc=1, device_id=t, device_id_type=pl.DeviceIdType.MESH)
    pl.semaphore_wait(bar, 3)

    def chunk(way, e, core):
        far = e // 2 + 1
        part = e % 2
        origin = lax.rem(z + (chips - far if way == 0 else far), chips)
        return pl.ds(pl.multiple_of(origin * chip + core * own + (part if way == 0 else 1 - part) * half, half), half)

    heads = (tok_h, cot_h)
    bufs = (tok, cot)

    def sent(s, way, e):
        return mesh_copy(bufs[s].at[chunk(way, e - 2, c)], bufs[s].at[chunk(way, e - 2, c)],
                         ring_send.at[s, way, e], ring_recv.at[s, way, e], side[way])

    def first(s, way, e):
        h = e if way == 0 else 1 - e
        return mesh_copy(heads[s].at[pl.ds(h * half, half)],
                         bufs[s].at[pl.ds(pl.multiple_of(me * own + h * half, half), half)],
                         ring_send.at[s, way, e], ring_recv.at[s, way, e], side[way])

    def shared(s, way, e):
        return mesh_copy(bufs[s].at[chunk(way, e, c)], bufs[s].at[chunk(way, e, c)],
                         sib_send.at[s, way, e], sib_recv.at[s, way, e], sib)

    place = pl.ds(pl.multiple_of(me * own, own), own)

    def lodged(s):
        return mesh_copy(heads[s], bufs[s].at[place], own_send.at[s], own_recv.at[s], sib)

    def kept(s):
        return pltpu.make_async_copy(heads[s], bufs[s].at[place], local.at[s])

    def begin(s):
        for e in (0, 1):
            for way in (0, 1):
                first(s, way, e).start()
        lodged(s).start()
        kept(s).start()

    def event(s, i):
        @pl.when(i < events)
        def _():
            for way in (0, 1):
                mesh_copy(bufs[s].at[chunk(way, i, c)], bufs[s].at[chunk(way, i, c)],
                          ring_send.at[s, way, i], ring_recv.at[s, way, i], side[way]).wait_recv()

                @pl.when(i < events - 2)
                def _():
                    sent(s, way, i + 2).start()
                shared(s, way, i).start()

    def block_row(s, i):
        far = (i + 1) // 2

        @pl.when(i == 0)
        def _():
            lodged(s).wait_recv()
            kept(s).wait()

        for way in (0, 1):
            @pl.when(jnp.logical_and(i % 2 == 1 - way, jnp.logical_and(i > 0, i < chips - 1)))
            def _():
                shared(s, way, 2 * far - 2).wait_recv()
                shared(s, way, 2 * far - 1).wait_recv()

            @pl.when(i == chips - 1)
            def _():
                shared(s, way, events - 1).wait_recv()
        zc = lax.rem(z + jnp.where(i % 2 == 1, chips - far, far), chips)
        return pl.multiple_of(zc * chip, chip)

    begin(0)
    for j in range(3):
        w[:, j * hd:(j + 1) * hd] = w3[j]
    lists = tiles[...]
    lane = lax.broadcasted_iota(jnp.int32, (hd, hd), 1)
    count = lists.shape[0]
    hit = jnp.zeros((count, hd), jnp.bool_)
    for j in range(lists.shape[1]):
        hit = jnp.logical_or(hit, lists[:, j:j + 1] == lane[:count])
    bias = jnp.where(hit, 0.0, -30000.0)
    bias = jnp.transpose(jnp.concatenate([bias, jnp.zeros((hd - count, hd), F32)], axis=0))
    for j in range(count):
        kn[j * tile_rows:(j + 1) * tile_rows, hd:] = jnp.broadcast_to(bias[j:j + 1, :], (tile_rows, hd)).astype(BF)
    dkt[...] = jnp.zeros_like(dkt)
    dvt[...] = jnp.zeros_like(dvt)

    @pl.loop(0, chips)
    def _(i):
        event(0, i)

        @pl.when(i == events - 3)
        def _():
            begin(1)
        row = block_row(0, i)
        qkv_block(row, chip, tok, w, gq, gk, qraw, kraw, qn, kn, va, tile_rows)

    @pl.loop(0, chips)
    def _(i):
        event(1, i)
        row = block_row(1, i)
        dA[pl.ds(row, chip), :] = mm(cot[pl.ds(row, chip), :], wo[...], 1, 1).astype(BF)
        attn_block(row, chip, None, scale, qn, kn, va, dA, qraw, gq, att_o, gl, dkt, dvt)

    gkc = jnp.transpose(jnp.broadcast_to(gk[...], (hd, hd)))[:, :1]
    finish(scale, kraw, gkc, dkt, dvt, gl)
    N = 256

    @pl.loop(0, tok.shape[1] // N)
    def _(i):
        col = pl.multiple_of(i * N, N)
        g_o[:3 * hd, pl.ds(col, N)] = mm(gl[...], tok[:, pl.ds(col, N)]).astype(BF)
        g_o[3 * hd:, pl.ds(col, N)] = mm(att_o[...], cot[:, pl.ds(col, N)], 0, 0).astype(BF)

    for s in (0, 1):
        lodged(s).wait_send()
        for way in (0, 1):
            for e in range(events):
                (first if e < 2 else sent)(s, way, e).wait_send()
                shared(s, way, e).wait_send()


def layer_call(n, hidden, cot, w3, wo, q_gain, k_gain, tiles):
    own, D = hidden.shape
    seq = own * n
    hd = q_gain.shape[0]
    V = pl.BlockSpec(memory_space=pltpu.VMEM)
    A = pl.BlockSpec(memory_space=pl.ANY)
    dma = pltpu.SemaphoreType.DMA
    e = n // 2 - 1
    return pl.pallas_call(
        functools.partial(layer_kernel, hd ** -0.5, n),
        out_shape=(jax.ShapeDtypeStruct((seq, hd), BF), jax.ShapeDtypeStruct((4 * hd, D), BF)),
        in_specs=[A, A] + [V] * 5, out_specs=(V, V),
        scratch_shapes=[pltpu.VMEM((seq, D), BF)] * 2 + [pltpu.VMEM((D, 3 * hd), BF)]
        + [pltpu.VMEM((seq, hd), F32)] * 2 + [pltpu.VMEM((seq, 2 * hd), BF)] * 3
        + [pltpu.VMEM((seq, hd), BF), pltpu.VMEM((3 * hd, seq), BF)] + [pltpu.VMEM((hd, seq), F32)] * 2
        + [dma((2, 2, e))] * 4 + [dma((2,))] * 3,
        compiler_params=pltpu.CompilerParams(collective_id=2, has_side_effects=True, vmem_limit_bytes=60 * 1024 * 1024),
    )(hidden, cot, w3, wo, q_gain[None], k_gain[None], tiles)


def exchange_kernel(n, m, att, w, g, out, gq_o, go_o, rows, send, recv, own, parts, full, rs_send, rs_recv, ag_send, ag_recv, gown):
    me = lax.axis_index("ctx"); dp = lax.axis_index("dp")
    T = rows.shape[0]; hd = att.shape[1]
    R = full.shape[0] // m
    bar = pltpu.get_barrier_semaphore()
    def peer(k):
        return lax.rem(me + k, n)
    def dpeer(k):
        return lax.rem(dp + k, m)
    for k in range(1, m):
        pl.semaphore_signal(bar, inc=1, device_id=(dpeer(k), me), device_id_type=pl.DeviceIdType.MESH)
    for k in range(1, n):
        pl.semaphore_signal(bar, inc=1, device_id=(dp, peer(k)), device_id_type=pl.DeviceIdType.MESH)
    pl.semaphore_wait(bar, n + m - 2)
    def band(p):
        return pl.ds(pl.multiple_of(p * R, R), R)
    def scatter(k):
        p = dpeer(k)
        return mesh_copy(g.at[band(p)], parts.at[k], rs_send.at[k], rs_recv.at[k], (p, me))
    def gather(k):
        return mesh_copy(full.at[band(dp)], full.at[band(dp)], ag_send.at[k], ag_recv.at[k], (dpeer(k), me))
    def copy(k):
        p = peer(k)
        return pltpu.make_async_remote_copy(
            src_ref=att.at[pl.ds(pl.multiple_of(p * T, T), T)],
            dst_ref=rows.at[:, pl.ds(pl.multiple_of(me * hd, hd), hd)],
            send_sem=send.at[k], recv_sem=recv.at[k],
            device_id=(dp, p), device_id_type=pl.DeviceIdType.MESH)
    for k in range(1, m):
        scatter(k).start()
    for k in range(1, n):
        copy(k).start()
    mine = pltpu.make_async_copy(att.at[pl.ds(pl.multiple_of(me * T, T), T)],
                                 rows.at[:, pl.ds(pl.multiple_of(me * hd, hd), hd)], own)
    mine.start()
    keep = pltpu.make_async_copy(g.at[band(dp)], parts.at[0], gown)
    keep.start()
    keep.wait()
    total = parts[0].astype(F32)
    for k in range(1, m):
        scatter(k).wait_recv()
        total = total + parts[k].astype(F32)
    full[band(dp), :] = total.astype(BF)
    for k in range(1, m):
        gather(k).start()
    mine.wait()
    for k in range(1, n):
        copy(k).wait()
    out[...] = mm(rows[...], w[...]).astype(BF)
    for k in range(1, m):
        gather(k).wait_recv()
    for j in range(3):
        gq_o[j] = jnp.transpose(full[j * hd:(j + 1) * hd, :].astype(F32))
    go_o[...] = full[3 * hd:, :].astype(F32)
    for k in range(1, m):
        scatter(k).wait_send()
        gather(k).wait_send()


def exchange_call(att, w_full, g, n, m):
    seq, hd = att.shape
    D = w_full.shape[1]
    V = pl.BlockSpec(memory_space=pltpu.VMEM)
    A = pl.BlockSpec(memory_space=pl.ANY)
    dma = pltpu.SemaphoreType.DMA
    return pl.pallas_call(functools.partial(exchange_kernel, n, m),
        out_shape=(jax.ShapeDtypeStruct((seq // n, D), BF), jax.ShapeDtypeStruct((3, D, hd), F32),
                   jax.ShapeDtypeStruct((hd, D), F32)),
        in_specs=[A, V, A], out_specs=(V, V, V),
        scratch_shapes=[pltpu.VMEM((seq // n, n * hd), BF), dma((n,)), dma((n,)), dma,
                        pltpu.VMEM((m, 4 * hd // m, D), BF), pltpu.VMEM((4 * hd, D), BF)]
        + [dma((m,))] * 4 + [dma],
        compiler_params=pltpu.CompilerParams(collective_id=1, has_side_effects=True, vmem_limit_bytes=40 * 1024 * 1024),
    )(att, w_full, g)


def per_device(n, m, hidden_in, cotangent, w_qkv, w_out, q_gain, k_gain, tile_list):
    w_full = lax.all_gather(w_out, "ctx", axis=0, tiled=True)
    att, g = layer_call(n, hidden_in[0], cotangent[0], w_qkv, w_out, q_gain, k_gain, tile_list[0])
    layer, gq, go = exchange_call(att, w_full, g, n, m)
    return layer[None], gq, go


def solution(mesh):
    in_specs = (
        P("dp", "ctx", None),
        P("dp", "ctx", None),
        P(None, None, "ctx"),
        P("ctx", None),
        P(),
        P(),
        P("ctx", None, None),
    )
    out_specs = (P("dp", "ctx", None), P(None, None, "ctx"), P("ctx", None))
    return jax.shard_map(
        functools.partial(per_device, mesh.shape["ctx"], mesh.shape["dp"]), mesh=mesh, in_specs=in_specs, out_specs=out_specs, check_vma=False
    )
```
